32 devices in a mesh: group: 4 (over z), node: 8 (over y, x, core).
Axes of the slice: x: 2, y: 2, z: 4, core: 2. Of those that a mesh axis runs over, the one named last changes fastest.
Arguments:
- tokens: bfloat16 [32, 4096], P(('group', 'node')), may hold values from -6 to 6
- expert_ids: int32 [32, 8], P(('group', 'node')), may hold values from 0 to 15, as said below
- route_scores: bfloat16 [32, 8], P(('group', 'node')), may hold values from -6 to 6
- gate_weight: bfloat16 [32, 4096, 512], P(('group', 'node')), may hold values from -0.09375 to 0.09375
- up_weight: bfloat16 [32, 4096, 512], P(('group', 'node')), may hold values from -0.09375 to 0.09375
- down_weight: bfloat16 [32, 512, 4096], P(('group', 'node')), may hold values from -0.1875 to 0.1875
Outputs:
- moe_output: bfloat16 [32, 4096], P(('group', 'node'))
The draws below stay inside these ranges and needn't reach their ends.
Inputs may be any that keep to these rules, and one draw needn't show every extreme that they name: `expert_ids`: expert e belongs to node group e // 4. Each token names 8 different experts, two in each of four different node groups. Among the tokens held by the devices with one index along node, every node group is named by exactly 4 tokens, no expert is named by more than 4 tokens, and in every node group one expert is named by exactly 4 of them.
All inputs are finite; a program needn't handle non-finite values.
Results may differ from the reference program's by a relative error of at most 0.0075.
Values may be sent and summed in bfloat16 or wider, within the bound.
A program may use at most 64 MiB of HBM per device.

```python
import jax
import jax.numpy as jnp
from jax import lax

D = 4096
FF = 1024
EXP_GROUP = 4
TOP = 8
TOK_DEV = 1
GROUPS = 4
SHARDS = 2
HID_DEV = 512
EXPERTS = 16
TOKENS = 32
SLOTS = 4


def draw_expert_ids(key, part):
    lane_tokens = GROUPS * TOK_DEV
    owners = SHARDS * EXP_GROUP
    key_hot, key_rest = jax.random.split(key)
    favored = jax.random.randint(key_hot, (GROUPS,), 0, EXP_GROUP)

    def one_lane(lane_key):
        key_one, key_two, key_three, key_four = jax.random.split(lane_key, 4)
        residue = jax.random.permutation(key_one, lane_tokens) % GROUPS
        table = jax.random.permutation(key_two, GROUPS)
        spacing = GROUPS // 4
        chosen = table[(residue[:, None] + spacing * jnp.arange(4)[None, :]) % GROUPS]
        offset = jax.random.randint(key_three, (lane_tokens, 4), 1, EXP_GROUP)
        first = favored[chosen]
        second = (first + offset) % EXP_GROUP
        named = jnp.stack([chosen * EXP_GROUP + first, chosen * EXP_GROUP + second], axis=2).reshape(lane_tokens, TOP)
        shuffle = jax.vmap(lambda inner_key: jax.random.permutation(inner_key, TOP))(jax.random.split(key_four, lane_tokens))
        return jnp.take_along_axis(named, shuffle, axis=1)
    lanes = jax.vmap(one_lane)(jax.random.split(key_rest, owners))
    lanes = lanes.reshape(owners, GROUPS, TOK_DEV, TOP).transpose(1, 0, 2, 3)
    return lanes.reshape(GROUPS * owners * TOK_DEV, TOP).astype(jnp.int32)


def block_scale(stream_key, dims, cuts, low, largest):
    factor_of = 1.0
    for dim, blocks in cuts:
        heights = jax.random.uniform(jax.random.fold_in(jax.random.fold_in(stream_key, 6), dim), (blocks,), jnp.float32, low / len(cuts), largest / len(cuts))
        factor_of = factor_of * jnp.repeat(jnp.exp(heights), dims[dim] // blocks).reshape((-1,) + (1,) * (len(dims) - 1 - dim))
    return factor_of


def gaussian(rng, shape, spread, most, shards=(), held_as=jnp.bfloat16):
    factor_of = block_scale(rng, shape, shards, -0.22, 0.18) if shards else 1.0
    drawn = jax.random.normal(rng, shape, jnp.float32) * spread * factor_of
    return jnp.minimum(jnp.maximum(drawn, -most), most).astype(held_as)


def setup_inputs(seed: int = 0) -> dict:
    key_list = jax.random.split(jax.random.key(seed), 7)
    tokens = gaussian(key_list[0], (TOKENS, D), 1.0, 6.0, ((0, 32),))
    expert_ids = draw_expert_ids(jax.random.fold_in(key_list[6], 71), 0)
    route_scores = gaussian(key_list[2], (TOKENS, TOP), 1.5, 6.0, ((0, 32),))
    gate_weight = gaussian(key_list[3], (EXPERTS * SHARDS, D, HID_DEV), D ** -0.5, 0.09375, ((0, 32),))
    up_weight = gaussian(key_list[4], (EXPERTS * SHARDS, D, HID_DEV), D ** -0.5, 0.09375, ((0, 32),))
    down_weight = gaussian(key_list[5], (EXPERTS * SHARDS, HID_DEV, D), FF ** -0.5, 0.1875, ((0, 32),))
    return {"tokens": tokens, "expert_ids": expert_ids, "route_scores": route_scores, "gate_weight": gate_weight, "up_weight": up_weight, "down_weight": down_weight}


ROUTE_SCALE = 2.5


def route_weights(route_scores):
    sigmoids = jax.nn.sigmoid(route_scores.astype(jnp.float32))
    return ROUTE_SCALE * sigmoids / jnp.sum(sigmoids, axis=1, keepdims=True)


def reference(tokens, expert_ids, route_scores, gate_weight, up_weight, down_weight):
    weights = route_weights(route_scores)
    capacity = SHARDS * EXP_GROUP * SLOTS
    width = tokens.shape[1]
    gate_all = gate_weight.reshape(EXPERTS, SHARDS, width, HID_DEV)
    up_all = up_weight.reshape(EXPERTS, SHARDS, width, HID_DEV)
    down_all = down_weight.reshape(EXPERTS, SHARDS, HID_DEV, width)

    def one_expert(totals, expert):
        matches = expert_ids == expert
        routed = jnp.any(matches, axis=1).astype(jnp.int32)
        shares = jnp.sum(jnp.where(matches, weights, jnp.zeros_like(weights)), axis=1)
        chosen = jnp.argsort(1 - routed, stable=True)[:capacity].astype(jnp.int32)
        picked = tokens[chosen]
        gates = lax.dynamic_index_in_dim(gate_all, expert, 0, keepdims=False)
        uppers = lax.dynamic_index_in_dim(up_all, expert, 0, keepdims=False)
        downs = lax.dynamic_index_in_dim(down_all, expert, 0, keepdims=False)
        summed = jnp.zeros((capacity, width), jnp.float32)
        for block_index in range(SHARDS):
            gate_pre = jnp.dot(picked, gates[block_index], preferred_element_type=jnp.float32)
            up_proj = jnp.dot(picked, uppers[block_index], preferred_element_type=jnp.float32)
            hidden = (jax.nn.silu(gate_pre) * up_proj).astype(jnp.bfloat16)
            partial_out = jnp.dot(hidden, downs[block_index], preferred_element_type=jnp.float32).astype(jnp.bfloat16)
            summed = summed + partial_out.astype(jnp.float32)
        totals = totals.at[chosen].add(shares[chosen][:, None] * summed)
        return totals, expert

    totals = jnp.zeros((tokens.shape[0], width), jnp.float32)
    totals, unused = lax.scan(one_expert, totals, jnp.arange(EXPERTS, dtype=jnp.int32))
    return totals.astype(jnp.bfloat16)
```

```python
import functools

import jax
import jax.numpy as jnp
from jax import lax
from jax.experimental import pallas as pl
from jax.experimental.pallas import tpu as pltpu
from jax.sharding import PartitionSpec as P

EXP_GROUP = 4


ROUTE_SCALE = 2.5


def route_weights(route_scores):
    sigmoids = jax.nn.sigmoid(route_scores.astype(jnp.float32))
    return ROUTE_SCALE * sigmoids / jnp.sum(sigmoids, axis=1, keepdims=True)


def expert_dense(arrived_rows, gate_weight, up_weight, down_weight):
    gate_pre = jnp.dot(arrived_rows, gate_weight[0], preferred_element_type=jnp.float32)
    up_proj = jnp.dot(arrived_rows, up_weight[0], preferred_element_type=jnp.float32)
    hidden = (jax.nn.silu(gate_pre) * up_proj).astype(jnp.bfloat16)
    return jnp.dot(hidden, down_weight[0], preferred_element_type=jnp.float32).astype(jnp.bfloat16)


def per_device(tokens, expert_ids, route_scores, gate_weight, up_weight, down_weight):
    local_tokens = tokens.shape[0]
    width = tokens.shape[1]
    slot_count = 4 * local_tokens
    gathered_rows, gathered_ids, gathered_scores = (
        lax.all_gather(tokens, "group", axis=0, tiled=True),
        lax.all_gather(expert_ids, "group", axis=0, tiled=True),
        lax.all_gather(route_scores, "group", axis=0, tiled=True),
    )
    route_share = route_weights(gathered_scores)
    arrived_count = gathered_rows.shape[0]
    local_ids = gathered_ids - lax.axis_index("group") * EXP_GROUP
    matches = local_ids[:, :, None] == jnp.arange(EXP_GROUP, dtype=jnp.int32)[None, None, :]
    routed = jnp.any(matches, axis=1)
    shares = jnp.sum(jnp.where(matches, route_share[:, :, None], 0.0), axis=1)
    row = jnp.arange(arrived_count, dtype=jnp.int32)
    earlier = (row[None, :] <= row[:, None])[:, :, None] & routed[None, :, :]
    ranking = jnp.sum(earlier.astype(jnp.int32), axis=1) - 1
    placing = routed[:, :, None] & (
        ranking[:, :, None] == jnp.arange(slot_count, dtype=jnp.int32)[None, None, :]
    )
    selector = placing.reshape(arrived_count, EXP_GROUP * slot_count).astype(jnp.bfloat16)
    per_expert = jnp.einsum(
        "rs,rd->sd", selector, gathered_rows, preferred_element_type=jnp.float32
    ).astype(jnp.bfloat16)
    shard_count = lax.axis_size("node") // EXP_GROUP
    outgoing = jnp.broadcast_to(
        per_expert.reshape(EXP_GROUP, 1, slot_count, width),
        (EXP_GROUP, shard_count, slot_count, width),
    ).reshape(EXP_GROUP * shard_count, slot_count, width)
    arrived = lax.all_to_all(outgoing, "node", split_axis=0, concat_axis=0, tiled=True)
    flat_rows = arrived.reshape(-1, width)
    produced = expert_dense(flat_rows, gate_weight, up_weight, down_weight)
    returned = lax.all_to_all(
        produced.reshape(arrived.shape), "node", split_axis=0, concat_axis=0, tiled=True
    )
    blocks = returned.reshape(EXP_GROUP, shard_count, slot_count, width)
    merged = jnp.zeros((EXP_GROUP, slot_count, width), jnp.float32)
    for shard_index in range(shard_count):
        merged = merged + blocks[:, shard_index].astype(jnp.float32)
    slot_index = jnp.clip(ranking, 0, slot_count - 1)
    group_rows = jnp.zeros((arrived_count, width), jnp.float32)
    for expert_local in range(EXP_GROUP):
        looked = merged[expert_local][slot_index[:, expert_local]]
        group_rows = group_rows + shares[:, expert_local][:, None] * looked
    summed = lax.psum_scatter(group_rows, "group", scatter_dimension=0, tiled=True)
    return summed.astype(jnp.bfloat16)


LANES = 128
CORES = 2
HALVES = 1
GROUPS_PER_TOKEN = 4
MESH = pl.DeviceIdType.MESH


def dense_kernel(
    groups, nodes, chunks,
    tokens_hbm, ids_hbm, scores_hbm, gate_hbm, up_hbm, down_hbm, out_ref,
    tokens_ref, ids_ref, scores_ref, gate_vmem, up_vmem, down_vmem, arrived, outgoing, mate, summed, returned, planes, rows_ref,
    weight_sems, token_send, token_recv, share_send, share_recv, part_sems, small_sems,
):
    devices = groups * nodes
    places = nodes // CORES
    chips = groups * places
    width = tokens_hbm.shape[1]
    hidden_size = gate_vmem.shape[1]
    lines = width // LANES
    depth = width // chunks
    group, node = lax.axis_index("group"), lax.axis_index("node")
    place, core = node // CORES, lax.rem(node, CORES)
    chip = group * places + place
    near = core * chips
    far = (1 - core) * chips
    sibling = (group, node + 1 - 2 * core)

    front_copies, down_copies = [], []
    for chunk in range(chunks):
        span = pl.ds(chunk * depth, depth)
        front_copies.append((
            pltpu.make_async_copy(gate_hbm.at[0, span, :], gate_vmem.at[span, :], weight_sems.at[0, chunk]),
            pltpu.make_async_copy(up_hbm.at[0, span, :], up_vmem.at[span, :], weight_sems.at[1, chunk]),
        ))
        down_copies.append(
            pltpu.make_async_copy(down_hbm.at[0, :, span], down_vmem.at[:, span], weight_sems.at[2, chunk]))
    def peer(step):
        other = lax.rem(chip + step, chips)
        return (other // places, lax.rem(other, places) * CORES + core)

    barrier = pltpu.get_barrier_semaphore()
    pl.semaphore_signal(barrier, inc=1, device_id=sibling, device_id_type=MESH)
    for step in range(1, chips):
        pl.semaphore_signal(barrier, inc=1, device_id=peer(step), device_id_type=MESH)

    small_copies = (
        pltpu.make_async_copy(tokens_hbm, tokens_ref, small_sems.at[0]),
        pltpu.make_async_copy(ids_hbm, ids_ref, small_sems.at[1]),
        pltpu.make_async_copy(scores_hbm, scores_ref, small_sems.at[2]),
    )
    for copy in small_copies:
        copy.start()
    for first, second in front_copies:
        first.start()
        second.start()
    for copy in down_copies:
        copy.start()
    for copy in small_copies:
        copy.wait()

    own = tokens_ref[...].astype(jnp.float32)
    for line in range(lines):
        planes[line:line + 1, :] = own[:, line * LANES:(line + 1) * LANES]
    arrived[near + chip] = planes[0:lines, :].astype(jnp.bfloat16)

    sigmoids = 1.0 / (1.0 + jnp.exp(-scores_ref[...].astype(jnp.float32)))
    weights = ROUTE_SCALE * sigmoids / jnp.sum(sigmoids, axis=1, keepdims=True)
    top = ids_ref.shape[1]
    chip_expert = lax.broadcasted_iota(jnp.int32, (chips, top), 0) // (nodes // EXP_GROUP // CORES)
    named = jnp.broadcast_to(ids_ref[...], (chips, top)) == chip_expert
    shares = jnp.sum(
        jnp.where(named, jnp.broadcast_to(weights, (chips, top)), 0.0), axis=1, keepdims=True)

    pl.semaphore_wait(barrier, chips)
    for step in range(1, chips):
        pltpu.make_async_remote_copy(
            src_ref=arrived.at[near + chip], dst_ref=arrived.at[near + chip],
            send_sem=token_send, recv_sem=token_recv.at[group],
            device_id=peer(step), device_id_type=MESH).start()
    forwards = []
    for step in range(groups):
        source = lax.rem(group + step, groups)
        count = places - 1 if step == 0 else places
        several = arrived.at[pl.ds(near + source * places, count)]
        pltpu.make_async_copy(several, several, token_recv.at[source]).wait()
        block = arrived.at[pl.ds(near + source * places, places)]
        forward = pltpu.make_async_remote_copy(
            src_ref=block, dst_ref=block,
            send_sem=share_send.at[step], recv_sem=share_recv.at[step],
            device_id=sibling, device_id_type=MESH)
        forward.start()
        forwards.append(forward)
    bulk = pl.ds(0, chips - 1)

    def lay_out(first_row, block):
        base = first_row * lines
        planes[base:base + chips * lines, :] = block.astype(jnp.float32).reshape(chips * lines, LANES)
        for line in range(lines):
            rows_ref[first_row:first_row + chips, line * LANES:(line + 1) * LANES] = planes[
                pl.ds(base + line, chips, stride=lines), :].astype(jnp.bfloat16)

    lay_out(0, arrived[pl.ds(near, chips)])
    for forward in forwards:
        forward.wait()
    lay_out(chips, arrived[pl.ds(far, chips)])

    gate_pre = jnp.zeros((devices, hidden_size), jnp.float32)
    up_proj = jnp.zeros((devices, hidden_size), jnp.float32)
    for chunk in range(chunks):
        span = slice(chunk * depth, (chunk + 1) * depth)
        front_copies[chunk][0].wait()
        front_copies[chunk][1].wait()
        rows = rows_ref[:, span]
        gate_pre += jnp.dot(rows, gate_vmem[span, :], preferred_element_type=jnp.float32)
        up_proj += jnp.dot(rows, up_vmem[span, :], preferred_element_type=jnp.float32)
    hidden = (gate_pre / (1.0 + jnp.exp(-gate_pre)) * up_proj).astype(jnp.bfloat16)

    half_lines = lines // HALVES
    span_rows = chips * half_lines
    swaps = []
    for chunk in range(chunks):
        down_copies[chunk].wait()
        part = jnp.dot(
            hidden, down_vmem[:, chunk * depth:(chunk + 1) * depth], preferred_element_type=jnp.float32)
        for piece in range(depth // LANES):
            line = chunk * (depth // LANES) + piece
            start = line // half_lines * CORES * span_rows + line % half_lines
            planes[pl.ds(start, devices, stride=half_lines), :] = part[:, piece * LANES:(piece + 1) * LANES]
        if (chunk + 1) % (chunks // HALVES) == 0:
            half = chunk // (chunks // HALVES)
            base = (half * CORES + 1) * span_rows
            outgoing[half] = planes[base:base + span_rows, :].astype(
                jnp.bfloat16).reshape(chips, half_lines, LANES)
            swap = pltpu.make_async_remote_copy(
                src_ref=outgoing.at[half], dst_ref=mate.at[half],
                send_sem=part_sems.at[0, half], recv_sem=part_sems.at[1, half],
                device_id=sibling, device_id_type=MESH)
            swap.start()
            swaps.append(swap)
    for half in range(HALVES):
        base = half * CORES * span_rows
        swaps[half].wait_recv()
        summed[half] = (
            planes[base:base + span_rows, :].reshape(chips, half_lines, LANES)
            + mate[half].astype(jnp.float32)).astype(jnp.bfloat16)
        for step in range(1, chips):
            pltpu.make_async_remote_copy(
                src_ref=summed.at[half, lax.rem(chip + step, chips)], dst_ref=returned.at[half, chip],
                send_sem=part_sems.at[2, half], recv_sem=part_sems.at[3, half],
                device_id=peer(step), device_id_type=MESH).start()
        returned[half, chip] = summed[half, chip]
    for half in range(HALVES):
        landed = returned.at[half, bulk]
        pltpu.make_async_copy(landed, landed, part_sems.at[3, half]).wait()
        total = jnp.zeros((half_lines, LANES), jnp.float32)
        for source in range(chips):
            total += shares[source:source + 1, :] * returned[half, source].astype(jnp.float32)
        out_ref[half * half_lines:(half + 1) * half_lines, :] = total.astype(jnp.bfloat16)
    pltpu.make_async_copy(arrived.at[bulk], arrived.at[bulk], token_send).wait()
    for half in range(HALVES):
        landed = returned.at[half, bulk]
        swaps[half].wait_send()
        pltpu.make_async_copy(landed, landed, part_sems.at[2, half]).wait()


def per_device_dense(groups, nodes, tokens, expert_ids, route_scores, gate_weight, up_weight, down_weight):
    devices = groups * nodes
    chips = devices // CORES
    width = tokens.shape[1]
    hidden_size = gate_weight.shape[2]
    lines = width // LANES
    chunks = 1
    parts = pltpu.VMEM((HALVES, chips, lines // HALVES, LANES), jnp.bfloat16)
    in_hbm = pl.BlockSpec(memory_space=pltpu.HBM)
    out = pl.pallas_call(
        functools.partial(dense_kernel, groups, nodes, chunks),
        out_shape=jax.ShapeDtypeStruct((lines, LANES), jnp.bfloat16),
        in_specs=[in_hbm] * 6,
        out_specs=pl.BlockSpec(memory_space=pltpu.VMEM),
        scratch_shapes=[
            pltpu.VMEM(tokens.shape, tokens.dtype),
            pltpu.VMEM(expert_ids.shape, expert_ids.dtype),
            pltpu.VMEM(route_scores.shape, route_scores.dtype),
            pltpu.VMEM((width, hidden_size), jnp.bfloat16),
            pltpu.VMEM((width, hidden_size), jnp.bfloat16),
            pltpu.VMEM((hidden_size, width), jnp.bfloat16),
            pltpu.VMEM((devices, lines, LANES), jnp.bfloat16),
            parts, parts, parts, parts,
            pltpu.VMEM((devices * lines, LANES), jnp.float32),
            pltpu.VMEM((devices, width), jnp.bfloat16),
            pltpu.SemaphoreType.DMA((3, chunks)),
            pltpu.SemaphoreType.DMA, pltpu.SemaphoreType.DMA((groups,)),
            pltpu.SemaphoreType.DMA((groups,)), pltpu.SemaphoreType.DMA((groups,)),
            pltpu.SemaphoreType.DMA((4, HALVES)), pltpu.SemaphoreType.DMA((3,)),
        ],
        compiler_params=pltpu.CompilerParams(
            collective_id=0, has_side_effects=True, vmem_limit_bytes=48 * 1024 * 1024),
    )(*(pltpu.with_memory_space_constraint(x, pltpu.HBM)
        for x in (tokens, expert_ids, route_scores, gate_weight, up_weight, down_weight)))
    return out.reshape(1, width)


def solution(mesh):
    groups, nodes = mesh.shape["group"], mesh.shape["node"]
    everyone = groups == GROUPS_PER_TOKEN
    body = functools.partial(per_device_dense, groups, nodes) if everyone else per_device
    return jax.shard_map(
        body,
        mesh=mesh,
        in_specs=(
            P(("group", "node"), None),
            P(("group", "node"), None),
            P(("group", "node"), None),
            P(("group", "node"), None, None),
            P(("group", "node"), None, None),
            P(("group", "node"), None, None),
        ),
        out_specs=P(("group", "node"), None),
        check_vma=False,
    )
```

```python
import functools

import jax
import jax.numpy as jnp
from jax import lax
from jax.experimental import pallas as pl
from jax.experimental.pallas import tpu as pltpu
from jax.sharding import PartitionSpec as P

EXP_GROUP = 4


ROUTE_SCALE = 2.5


def route_weights(route_scores):
    sigmoids = jax.nn.sigmoid(route_scores.astype(jnp.float32))
    return ROUTE_SCALE * sigmoids / jnp.sum(sigmoids, axis=1, keepdims=True)


def expert_dense(arrived_rows, gate_weight, up_weight, down_weight):
    gate_pre = jnp.dot(arrived_rows, gate_weight[0], preferred_element_type=jnp.float32)
    up_proj = jnp.dot(arrived_rows, up_weight[0], preferred_element_type=jnp.float32)
    hidden = (jax.nn.silu(gate_pre) * up_proj).astype(jnp.bfloat16)
    return jnp.dot(hidden, down_weight[0], preferred_element_type=jnp.float32).astype(jnp.bfloat16)


def per_device(tokens, expert_ids, route_scores, gate_weight, up_weight, down_weight):
    local_tokens = tokens.shape[0]
    width = tokens.shape[1]
    slot_count = 4 * local_tokens
    gathered_rows, gathered_ids, gathered_scores = (
        lax.all_gather(tokens, "group", axis=0, tiled=True),
        lax.all_gather(expert_ids, "group", axis=0, tiled=True),
        lax.all_gather(route_scores, "group", axis=0, tiled=True),
    )
    route_share = route_weights(gathered_scores)
    arrived_count = gathered_rows.shape[0]
    local_ids = gathered_ids - lax.axis_index("group") * EXP_GROUP
    matches = local_ids[:, :, None] == jnp.arange(EXP_GROUP, dtype=jnp.int32)[None, None, :]
    routed = jnp.any(matches, axis=1)
    shares = jnp.sum(jnp.where(matches, route_share[:, :, None], 0.0), axis=1)
    row = jnp.arange(arrived_count, dtype=jnp.int32)
    earlier = (row[None, :] <= row[:, None])[:, :, None] & routed[None, :, :]
    ranking = jnp.sum(earlier.astype(jnp.int32), axis=1) - 1
    placing = routed[:, :, None] & (
        ranking[:, :, None] == jnp.arange(slot_count, dtype=jnp.int32)[None, None, :]
    )
    selector = placing.reshape(arrived_count, EXP_GROUP * slot_count).astype(jnp.bfloat16)
    per_expert = jnp.einsum(
        "rs,rd->sd", selector, gathered_rows, preferred_element_type=jnp.float32
    ).astype(jnp.bfloat16)
    shard_count = lax.axis_size("node") // EXP_GROUP
    outgoing = jnp.broadcast_to(
        per_expert.reshape(EXP_GROUP, 1, slot_count, width),
        (EXP_GROUP, shard_count, slot_count, width),
    ).reshape(EXP_GROUP * shard_count, slot_count, width)
    arrived = lax.all_to_all(outgoing, "node", split_axis=0, concat_axis=0, tiled=True)
    flat_rows = arrived.reshape(-1, width)
    produced = expert_dense(flat_rows, gate_weight, up_weight, down_weight)
    returned = lax.all_to_all(
        produced.reshape(arrived.shape), "node", split_axis=0, concat_axis=0, tiled=True
    )
    blocks = returned.reshape(EXP_GROUP, shard_count, slot_count, width)
    merged = jnp.zeros((EXP_GROUP, slot_count, width), jnp.float32)
    for shard_index in range(shard_count):
        merged = merged + blocks[:, shard_index].astype(jnp.float32)
    slot_index = jnp.clip(ranking, 0, slot_count - 1)
    group_rows = jnp.zeros((arrived_count, width), jnp.float32)
    for expert_local in range(EXP_GROUP):
        looked = merged[expert_local][slot_index[:, expert_local]]
        group_rows = group_rows + shares[:, expert_local][:, None] * looked
    summed = lax.psum_scatter(group_rows, "group", scatter_dimension=0, tiled=True)
    return summed.astype(jnp.bfloat16)


LANES = 128
CORES = 2
SIDE = 2
GROUPS_PER_TOKEN = 4
MESH = pl.DeviceIdType.MESH
PEERS = (
    (0, 1, 1), (0, 1, 0), (0, 0, 1), (1, 1, 1), (0, 0, 0), (1, 1, 0), (1, 0, 1), (2, 1, 1),
    (1, 0, 0), (2, 1, 0), (2, 0, 1), (3, 1, 1), (2, 0, 0), (3, 1, 0), (3, 0, 1),
)


def dense_kernel(
    groups, nodes,
    tokens_hbm, ids_hbm, scores_hbm, gate_hbm, up_hbm, down_hbm, out_ref,
    tokens_ref, ids_ref, scores_ref, gate_vmem, up_vmem, down_vmem,
    arrived, outgoing, mate, summed, returned, planes, rows_ref,
    weight_sems, small_sems, token_send, token_recv, share_recv, swap_sems, part_send, part_recv,
):
    devices = groups * nodes
    places = nodes // CORES
    chips = groups * places
    width = tokens_hbm.shape[1]
    lines = width // LANES
    group, node = lax.axis_index("group"), lax.axis_index("node")
    place, core = node // CORES, lax.rem(node, CORES)
    row, column = place // SIDE, lax.rem(place, SIDE)
    chip = group * places + place
    near = core * chips
    far = (1 - core) * chips
    sibling = (group, node + 1 - 2 * core)
    low = (groups - 1 - group) // 2
    farthest_first = (3 * low, 1 + low, low * (1 - group) + (1 - low) * (5 - group), group)

    def peer(code):
        rank, turn_row, turn_column = code
        other_row = row + turn_row - 2 * row * turn_row
        other_column = column + turn_column - 2 * column * turn_column
        return farthest_first[rank], other_row * SIDE + other_column

    spots = [peer(code) for code in PEERS]
    chip_of = [level * places + spot for level, spot in spots]

    def device(index, other_core):
        level, spot = spots[index]
        return (level, spot * CORES + other_core)

    weight_copies = (
        pltpu.make_async_copy(gate_hbm.at[0], gate_vmem, weight_sems.at[0]),
        pltpu.make_async_copy(up_hbm.at[0], up_vmem, weight_sems.at[1]),
        pltpu.make_async_copy(down_hbm.at[0], down_vmem, weight_sems.at[2]),
    )

    barrier = pltpu.get_barrier_semaphore()

    def greet(target):
        pl.semaphore_signal(barrier, inc=1, device_id=target, device_id_type=MESH)

    for index in range(chips - 1):
        greet(device(index, core))
    greet(sibling)

    small_copies = (
        pltpu.make_async_copy(tokens_hbm, tokens_ref, small_sems.at[0]),
        pltpu.make_async_copy(ids_hbm, ids_ref, small_sems.at[1]),
        pltpu.make_async_copy(scores_hbm, scores_ref, small_sems.at[2]),
    )
    for copy in small_copies:
        copy.start()
    for copy in weight_copies:
        copy.start()
    for copy in small_copies:
        copy.wait()

    own = tokens_ref[...].astype(jnp.float32)
    for line in range(lines):
        planes[line:line + 1, :] = own[:, line * LANES:(line + 1) * LANES]
    arrived[near + chip] = planes[0:lines, :].astype(jnp.bfloat16)

    sigmoids = 1.0 / (1.0 + jnp.exp(-scores_ref[...].astype(jnp.float32)))
    weights = ROUTE_SCALE * sigmoids / jnp.sum(sigmoids, axis=1, keepdims=True)
    top = ids_ref.shape[1]
    source_chip = lax.broadcasted_iota(jnp.int32, (chips, top), 0)
    source_expert = source_chip // (nodes // EXP_GROUP // CORES)
    named = jnp.broadcast_to(ids_ref[...], (chips, top)) == source_expert
    shares = jnp.sum(
        jnp.where(named, jnp.broadcast_to(weights, (chips, top)), 0.0), axis=1, keepdims=True)

    pl.semaphore_wait(barrier, chips)

    def send_token(slot, receive, target):
        pltpu.make_async_remote_copy(
            src_ref=arrived.at[slot], dst_ref=arrived.at[slot],
            send_sem=token_send, recv_sem=receive,
            device_id=target, device_id_type=MESH).start()

    for index in range(chips - 1):
        send_token(near + chip, token_recv.at[chip], device(index, core))
    send_token(near + chip, share_recv, sibling)
    for index in reversed(range(chips - 1)):
        slot = near + chip_of[index]
        landed = arrived.at[slot]
        pltpu.make_async_copy(landed, landed, token_recv.at[chip_of[index]]).wait()
        send_token(slot, share_recv, sibling)

    def lay_out(first_row, block):
        base = first_row * lines
        planes[base:base + chips * lines, :] = block.astype(jnp.float32).reshape(chips * lines, LANES)
        for line in range(lines):
            rows_ref[first_row:first_row + chips, line * LANES:(line + 1) * LANES] = planes[
                pl.ds(base + line, chips, stride=lines), :].astype(jnp.bfloat16)

    lay_out(0, arrived[pl.ds(near, chips)])
    shared = arrived.at[pl.ds(far, chips)]
    pltpu.make_async_copy(shared, shared, share_recv).wait()
    lay_out(chips, arrived[pl.ds(far, chips)])

    weight_copies[0].wait()
    weight_copies[1].wait()
    rows = rows_ref[...]
    gate_pre = jnp.dot(rows, gate_vmem[...], preferred_element_type=jnp.float32)
    up_proj = jnp.dot(rows, up_vmem[...], preferred_element_type=jnp.float32)
    hidden = (gate_pre / (1.0 + jnp.exp(-gate_pre)) * up_proj).astype(jnp.bfloat16)

    span_rows = chips * lines
    weight_copies[2].wait()
    part = jnp.dot(hidden, down_vmem[...], preferred_element_type=jnp.float32)
    for line in range(lines):
        planes[pl.ds(line, devices, stride=lines), :] = part[:, line * LANES:(line + 1) * LANES]

    def own_part(index):
        return planes[pl.ds(pl.multiple_of(chip_of[index] * lines, lines), lines), :]

    def send_part(index):
        pltpu.make_async_remote_copy(
            src_ref=summed.at[chip_of[index]], dst_ref=returned.at[chip],
            send_sem=part_send, recv_sem=part_recv,
            device_id=device(index, core), device_id_type=MESH).start()

    def send_near(index):
        summed[chip_of[index]] = (
            own_part(index) + mate[chip_of[index]].astype(jnp.float32)).astype(jnp.bfloat16)
        send_part(index)

    outgoing[...] = planes[span_rows:2 * span_rows, :].astype(jnp.bfloat16).reshape(chips, lines, LANES)
    swap = pltpu.make_async_remote_copy(
        src_ref=outgoing, dst_ref=mate, send_sem=swap_sems.at[0], recv_sem=swap_sems.at[1],
        device_id=sibling, device_id_type=MESH)
    swap.start()
    swap.wait_recv()
    for index in range(chips - 1):
        send_near(index)
    returned[chip] = (
        planes[pl.ds(pl.multiple_of(chip * lines, lines), lines), :]
        + mate[chip].astype(jnp.float32)).astype(jnp.bfloat16)
    bulk = pl.ds(0, chips - 1)

    landed = returned.at[bulk]
    pltpu.make_async_copy(landed, landed, part_recv).wait()
    total = jnp.zeros((lines, LANES), jnp.float32)
    for source in range(chips):
        total += shares[source:source + 1, :] * returned[source].astype(jnp.float32)
    out_ref[...] = total.astype(jnp.bfloat16)
    sent = arrived.at[pl.ds(0, devices - 1)]
    pltpu.make_async_copy(sent, sent, token_send).wait()
    swap.wait_send()
    pltpu.make_async_copy(landed, landed, part_send).wait()


def per_device_dense(groups, nodes, tokens, expert_ids, route_scores, gate_weight, up_weight, down_weight):
    devices = groups * nodes
    chips = devices // CORES
    width = tokens.shape[1]
    hidden_size = gate_weight.shape[2]
    lines = width // LANES
    parts = pltpu.VMEM((chips, lines, LANES), jnp.bfloat16)
    in_hbm = pl.BlockSpec(memory_space=pltpu.HBM)
    dma = pltpu.SemaphoreType.DMA
    out = pl.pallas_call(
        functools.partial(dense_kernel, groups, nodes),
        out_shape=jax.ShapeDtypeStruct((lines, LANES), jnp.bfloat16),
        in_specs=[in_hbm] * 6,
        out_specs=pl.BlockSpec(memory_space=pltpu.VMEM),
        scratch_shapes=[
            pltpu.VMEM(tokens.shape, tokens.dtype),
            pltpu.VMEM(expert_ids.shape, expert_ids.dtype),
            pltpu.VMEM(route_scores.shape, route_scores.dtype),
            pltpu.VMEM((width, hidden_size), jnp.bfloat16),
            pltpu.VMEM((width, hidden_size), jnp.bfloat16),
            pltpu.VMEM((hidden_size, width), jnp.bfloat16),
            pltpu.VMEM((devices, lines, LANES), jnp.bfloat16),
            parts, parts, parts, parts,
            pltpu.VMEM((devices * lines, LANES), jnp.float32),
            pltpu.VMEM((devices, width), jnp.bfloat16),
            dma((3,)), dma((3,)), dma, dma((chips,)), dma, dma((2,)), dma, dma,
        ],
        compiler_params=pltpu.CompilerParams(
            collective_id=0, has_side_effects=True, vmem_limit_bytes=48 * 1024 * 1024),
    )(*(pltpu.with_memory_space_constraint(x, pltpu.HBM)
        for x in (tokens, expert_ids, route_scores, gate_weight, up_weight, down_weight)))
    return out.reshape(1, width)


def solution(mesh):
    groups, nodes = mesh.shape["group"], mesh.shape["node"]
    everyone = groups == GROUPS_PER_TOKEN and nodes == CORES * SIDE * SIDE
    body = functools.partial(per_device_dense, groups, nodes) if everyone else per_device
    return jax.shard_map(
        body,
        mesh=mesh,
        in_specs=(
            P(("group", "node"), None),
            P(("group", "node"), None),
            P(("group", "node"), None),
            P(("group", "node"), None, None),
            P(("group", "node"), None, None),
            P(("group", "node"), None, None),
        ),
        out_specs=P(("group", "node"), None),
        check_vma=False,
    )
```

```python
import functools

import jax
import jax.numpy as jnp
from jax import lax
from jax.experimental import pallas as pl
from jax.experimental.pallas import tpu as pltpu
from jax.sharding import PartitionSpec as P

EXP_GROUP = 4


ROUTE_SCALE = 2.5


def route_weights(route_scores):
    sigmoids = jax.nn.sigmoid(route_scores.astype(jnp.float32))
    return ROUTE_SCALE * sigmoids / jnp.sum(sigmoids, axis=1, keepdims=True)


def expert_dense(arrived_rows, gate_weight, up_weight, down_weight):
    gate_pre = jnp.dot(arrived_rows, gate_weight[0], preferred_element_type=jnp.float32)
    up_proj = jnp.dot(arrived_rows, up_weight[0], preferred_element_type=jnp.float32)
    hidden = (jax.nn.silu(gate_pre) * up_proj).astype(jnp.bfloat16)
    return jnp.dot(hidden, down_weight[0], preferred_element_type=jnp.float32).astype(jnp.bfloat16)


def per_device(tokens, expert_ids, route_scores, gate_weight, up_weight, down_weight):
    local_tokens = tokens.shape[0]
    width = tokens.shape[1]
    slot_count = 4 * local_tokens
    gathered_rows, gathered_ids, gathered_scores = (
        lax.all_gather(tokens, "group", axis=0, tiled=True),
        lax.all_gather(expert_ids, "group", axis=0, tiled=True),
        lax.all_gather(route_scores, "group", axis=0, tiled=True),
    )
    route_share = route_weights(gathered_scores)
    arrived_count = gathered_rows.shape[0]
    local_ids = gathered_ids - lax.axis_index("group") * EXP_GROUP
    matches = local_ids[:, :, None] == jnp.arange(EXP_GROUP, dtype=jnp.int32)[None, None, :]
    routed = jnp.any(matches, axis=1)
    shares = jnp.sum(jnp.where(matches, route_share[:, :, None], 0.0), axis=1)
    row = jnp.arange(arrived_count, dtype=jnp.int32)
    earlier = (row[None, :] <= row[:, None])[:, :, None] & routed[None, :, :]
    ranking = jnp.sum(earlier.astype(jnp.int32), axis=1) - 1
    placing = routed[:, :, None] & (
        ranking[:, :, None] == jnp.arange(slot_count, dtype=jnp.int32)[None, None, :]
    )
    selector = placing.reshape(arrived_count, EXP_GROUP * slot_count).astype(jnp.bfloat16)
    per_expert = jnp.einsum(
        "rs,rd->sd", selector, gathered_rows, preferred_element_type=jnp.float32
    ).astype(jnp.bfloat16)
    shard_count = lax.axis_size("node") // EXP_GROUP
    outgoing = jnp.broadcast_to(
        per_expert.reshape(EXP_GROUP, 1, slot_count, width),
        (EXP_GROUP, shard_count, slot_count, width),
    ).reshape(EXP_GROUP * shard_count, slot_count, width)
    arrived = lax.all_to_all(outgoing, "node", split_axis=0, concat_axis=0, tiled=True)
    flat_rows = arrived.reshape(-1, width)
    produced = expert_dense(flat_rows, gate_weight, up_weight, down_weight)
    returned = lax.all_to_all(
        produced.reshape(arrived.shape), "node", split_axis=0, concat_axis=0, tiled=True
    )
    blocks = returned.reshape(EXP_GROUP, shard_count, slot_count, width)
    merged = jnp.zeros((EXP_GROUP, slot_count, width), jnp.float32)
    for shard_index in range(shard_count):
        merged = merged + blocks[:, shard_index].astype(jnp.float32)
    slot_index = jnp.clip(ranking, 0, slot_count - 1)
    group_rows = jnp.zeros((arrived_count, width), jnp.float32)
    for expert_local in range(EXP_GROUP):
        looked = merged[expert_local][slot_index[:, expert_local]]
        group_rows = group_rows + shares[:, expert_local][:, None] * looked
    summed = lax.psum_scatter(group_rows, "group", scatter_dimension=0, tiled=True)
    return summed.astype(jnp.bfloat16)


LANES = 128
CORES = 2
SIDE = 2
GROUPS_PER_TOKEN = 4
MESH = pl.DeviceIdType.MESH
ACROSS = (
    (0, 1, 1), (0, 1, 0), (0, 0, 1), (1, 1, 1), (0, 0, 0), (1, 1, 0), (1, 0, 1), (1, 0, 0),
)
BESIDE = ((2, 1, 1), (3, 1, 1), (2, 1, 0), (2, 0, 1), (2, 0, 0), (3, 1, 0), (3, 0, 1))


def dense_kernel(
    groups, nodes,
    tokens_hbm, ids_hbm, scores_hbm, gate_hbm, up_hbm, down_hbm, out_ref,
    tokens_ref, ids_ref, scores_ref, gate_vmem, up_vmem, down_vmem,
    arrived, outgoing, mate, summed, returned, planes, rows_ref,
    weight_sems, small_sems, token_send, token_recv, own_recv, share_recv,
    swap_sems, part_send, part_recv, own_part_recv,
):
    devices = groups * nodes
    places = nodes // CORES
    chips = groups * places
    half = chips // 2
    width = tokens_hbm.shape[1]
    lines = width // LANES
    group, node = lax.axis_index("group"), lax.axis_index("node")
    place, core = node // CORES, lax.rem(node, CORES)
    row, column = place // SIDE, lax.rem(place, SIDE)
    chip = group * places + place
    me = group * nodes + node
    sibling = (group, node + 1 - 2 * core)
    low = (groups - 1 - group) // 2
    levels = (3 * low, 1 + low, low * (1 - group) + (1 - low) * (5 - group), group)
    hub_start = (core * low + (1 - core) * (1 - low)) * chips
    other_start = (core * (1 - low) + (1 - core) * low) * chips

    def locate(code):
        rank, turn_row, turn_column = code
        other_row = row + turn_row - 2 * row * turn_row
        other_column = column + turn_column - 2 * column * turn_column
        return levels[rank], other_row * SIDE + other_column

    across = [locate(code) for code in ACROSS]
    beside = [locate(code) for code in BESIDE]

    def device(spot, other_core):
        return (spot[0], spot[1] * CORES + other_core)

    def seat(spot):
        return lax.rem(spot[0] * places + spot[1], half)

    def by_core(second, first):
        pl.when(core == 1)(second)
        pl.when(core == 0)(first)

    weight_copies = (
        pltpu.make_async_copy(gate_hbm.at[0], gate_vmem, weight_sems.at[0]),
        pltpu.make_async_copy(up_hbm.at[0], up_vmem, weight_sems.at[1]),
        pltpu.make_async_copy(down_hbm.at[0], down_vmem, weight_sems.at[2]),
    )

    barrier = pltpu.get_barrier_semaphore()

    def greet(targets):
        for target in targets:
            pl.semaphore_signal(barrier, inc=1, device_id=target, device_id_type=MESH)

    greet([device(spot, 1) for spot in across])
    by_core(
        lambda: greet([device(spot, 0) for spot in across]),
        lambda: greet([device(spot, 1) for spot in beside]))
    greet([device(spot, 0) for spot in beside] + [sibling])
    greeted = 2 * (chips - 1 - half) + half + 1 + core

    small_copies = (
        pltpu.make_async_copy(tokens_hbm, tokens_ref, small_sems.at[0]),
        pltpu.make_async_copy(ids_hbm, ids_ref, small_sems.at[1]),
        pltpu.make_async_copy(scores_hbm, scores_ref, small_sems.at[2]),
    )
    for copy in small_copies:
        copy.start()
    weight_copies[0].start(priority=1)
    weight_copies[1].start(priority=1)
    for copy in small_copies:
        copy.wait()

    own = tokens_ref[...].astype(jnp.float32)
    for line in range(lines):
        planes[line:line + 1, :] = own[:, line * LANES:(line + 1) * LANES]
    arrived[me] = planes[0:lines, :].astype(jnp.bfloat16)

    sigmoids = 1.0 / (1.0 + jnp.exp(-scores_ref[...].astype(jnp.float32)))
    weights = ROUTE_SCALE * sigmoids / jnp.sum(sigmoids, axis=1, keepdims=True)
    top = ids_ref.shape[1]
    chip_expert = lax.broadcasted_iota(jnp.int32, (chips, top), 0) // (nodes // EXP_GROUP // CORES)
    named = jnp.broadcast_to(ids_ref[...], (chips, top)) == chip_expert
    shares = jnp.sum(
        jnp.where(named, jnp.broadcast_to(weights, (chips, top)), 0.0), axis=1, keepdims=True)

    pl.semaphore_wait(barrier, greeted)

    def send_tokens(ref, receive, target):
        pltpu.make_async_remote_copy(
            src_ref=ref, dst_ref=ref, send_sem=token_send, recv_sem=receive,
            device_id=target, device_id_type=MESH).start()

    for spot in across:
        send_tokens(arrived.at[me], token_recv.at[lax.rem(chip, half)], device(spot, 1))
    for spot in beside:
        send_tokens(arrived.at[me], token_recv.at[lax.rem(chip, half)], device(spot, 0))
    send_tokens(arrived.at[me], own_recv, sibling)
    weight_copies[2].start(priority=1)

    def pass_on(spots):
        for spot in reversed(spots):
            pair = arrived.at[pl.ds((spot[0] * places + spot[1]) * CORES, CORES)]
            pltpu.make_async_copy(pair, pair, token_recv.at[seat(spot)]).wait()
            send_tokens(pair, share_recv, sibling)

    by_core(lambda: pass_on(across), lambda: pass_on(beside))

    def wait_for(ref, semaphore):
        pltpu.make_async_copy(ref, ref, semaphore).wait()

    def lay_out(first, start):
        planes[first * lines:(first + chips) * lines, :] = arrived[
            pl.ds(start, chips)].astype(jnp.float32).reshape(chips * lines, LANES)
        for line in range(lines):
            rows_ref[first:first + chips, line * LANES:(line + 1) * LANES] = planes[
                pl.ds(first * lines + line, chips, stride=lines), :].astype(jnp.bfloat16)

    def product(left, right):
        return jnp.dot(left, right, preferred_element_type=jnp.float32)

    def front(first):
        rows = rows_ref[first:first + chips, :]
        gate_pre, up_proj = product(rows, gate_vmem[...]), product(rows, up_vmem[...])
        return (gate_pre / (1.0 + jnp.exp(-gate_pre)) * up_proj).astype(jnp.bfloat16)

    def back(first, hidden):
        produced = product(hidden, down_vmem[...])
        for line in range(lines):
            planes[pl.ds(first * lines + line, chips, stride=lines), :] = produced[:, line * LANES:(line + 1) * LANES]

    wait_for(arrived.at[0], own_recv)
    lay_out(0, hub_start)
    weight_copies[0].wait()
    weight_copies[1].wait()
    hub_hidden = front(0)
    by_core(
        lambda: wait_for(arrived.at[pl.ds(0, chips - CORES)], share_recv),
        lambda: wait_for(arrived.at[pl.ds(0, chips)], share_recv))
    lay_out(chips, other_start)
    other_hidden = front(chips)
    weight_copies[2].wait()
    back(chips, other_hidden)
    outgoing[...] = planes[chips * lines:2 * chips * lines, :].astype(jnp.bfloat16).reshape(chips, lines, LANES)
    swap = pltpu.make_async_remote_copy(
        src_ref=outgoing, dst_ref=mate, send_sem=swap_sems.at[0], recv_sem=swap_sems.at[1],
        device_id=sibling, device_id_type=MESH)
    swap.start()
    back(0, hub_hidden)
    swap.wait_recv()

    def add_up(base, count):
        begin = pl.multiple_of(base * lines, lines)
        return (
            planes[pl.ds(begin, count * lines), :].reshape(count, lines, LANES)
            + mate[pl.ds(base, count)].astype(jnp.float32)).astype(jnp.bfloat16)

    def send_part(index, receive, target):
        pltpu.make_async_remote_copy(
            src_ref=summed.at[index], dst_ref=returned.at[chip],
            send_sem=part_send, recv_sem=receive,
            device_id=target, device_id_type=MESH).start()

    def give_back(spots):
        for spot in spots:
            base = seat(spot) * CORES
            summed[pl.ds(base, CORES)] = add_up(base, CORES)
            for other_core in range(CORES):
                send_part(base + other_core, part_recv, device(spot, other_core))

    def give_back_beside():
        give_back(beside)
        base = lax.rem(chip, half) * CORES
        summed[pl.ds(base, CORES)] = add_up(base, CORES)
        send_part(base + 1, own_part_recv, sibling)
        returned[chip] = summed[base]

    by_core(lambda: give_back(across), give_back_beside)
    wait_for(returned.at[pl.ds(0, chips - 1)], part_recv)
    pl.when(core == 1)(lambda: wait_for(returned.at[0], own_part_recv))
    total = jnp.zeros((lines, LANES), jnp.float32)
    for source in range(chips):
        total += shares[source:source + 1, :] * returned[source].astype(jnp.float32)
    out_ref[...] = total.astype(jnp.bfloat16)
    swap.wait_send()

    def drain(tokens_sent, parts_sent):
        wait_for(arrived.at[pl.ds(0, tokens_sent)], token_send)
        wait_for(returned.at[pl.ds(0, parts_sent)], part_send)

    by_core(lambda: drain(devices, chips), lambda: drain(devices - CORES, chips - 1))


def per_device_dense(groups, nodes, tokens, expert_ids, route_scores, gate_weight, up_weight, down_weight):
    devices = groups * nodes
    chips = devices // CORES
    width = tokens.shape[1]
    hidden_size = gate_weight.shape[2]
    lines = width // LANES
    parts = pltpu.VMEM((chips, lines, LANES), jnp.bfloat16)
    in_hbm = pl.BlockSpec(memory_space=pltpu.HBM)
    dma = pltpu.SemaphoreType.DMA
    out = pl.pallas_call(
        functools.partial(dense_kernel, groups, nodes),
        out_shape=jax.ShapeDtypeStruct((lines, LANES), jnp.bfloat16),
        in_specs=[in_hbm] * 6,
        out_specs=pl.BlockSpec(memory_space=pltpu.VMEM),
        scratch_shapes=[
            pltpu.VMEM(tokens.shape, tokens.dtype),
            pltpu.VMEM(expert_ids.shape, expert_ids.dtype),
            pltpu.VMEM(route_scores.shape, route_scores.dtype),
            pltpu.VMEM((width, hidden_size), jnp.bfloat16),
            pltpu.VMEM((width, hidden_size), jnp.bfloat16),
            pltpu.VMEM((hidden_size, width), jnp.bfloat16),
            pltpu.VMEM((devices, lines, LANES), jnp.bfloat16),
            parts, parts, parts, parts,
            pltpu.VMEM((devices * lines, LANES), jnp.float32),
            pltpu.VMEM((devices, width), jnp.bfloat16),
            dma((3,)), dma((3,)), dma, dma((chips // 2,)), dma, dma, dma((2,)), dma, dma, dma,
        ],
        compiler_params=pltpu.CompilerParams(
            collective_id=0, has_side_effects=True, vmem_limit_bytes=48 * 1024 * 1024),
    )(*(pltpu.with_memory_space_constraint(x, pltpu.HBM)
        for x in (tokens, expert_ids, route_scores, gate_weight, up_weight, down_weight)))
    return out.reshape(1, width)


def solution(mesh):
    groups, nodes = mesh.shape["group"], mesh.shape["node"]
    everyone = groups == GROUPS_PER_TOKEN and nodes == CORES * SIDE * SIDE
    body = functools.partial(per_device_dense, groups, nodes) if everyone else per_device
    return jax.shard_map(
        body,
        mesh=mesh,
        in_specs=(
            P(("group", "node"), None),
            P(("group", "node"), None),
            P(("group", "node"), None),
            P(("group", "node"), None, None),
            P(("group", "node"), None, None),
            P(("group", "node"), None, None),
        ),
        out_specs=P(("group", "node"), None),
        check_vma=False,
    )
```

```python
import functools

import jax
import jax.numpy as jnp
from jax import lax
from jax.experimental import pallas as pl
from jax.experimental.pallas import tpu as pltpu
from jax.sharding import PartitionSpec as P

EXP_GROUP = 4


ROUTE_SCALE = 2.5


def route_weights(route_scores):
    sigmoids = jax.nn.sigmoid(route_scores.astype(jnp.float32))
    return ROUTE_SCALE * sigmoids / jnp.sum(sigmoids, axis=1, keepdims=True)


def expert_dense(arrived_rows, gate_weight, up_weight, down_weight):
    gate_pre = jnp.dot(arrived_rows, gate_weight[0], preferred_element_type=jnp.float32)
    up_proj = jnp.dot(arrived_rows, up_weight[0], preferred_element_type=jnp.float32)
    hidden = (jax.nn.silu(gate_pre) * up_proj).astype(jnp.bfloat16)
    return jnp.dot(hidden, down_weight[0], preferred_element_type=jnp.float32).astype(jnp.bfloat16)


def per_device(tokens, expert_ids, route_scores, gate_weight, up_weight, down_weight):
    local_tokens = tokens.shape[0]
    width = tokens.shape[1]
    slot_count = 4 * local_tokens
    gathered_rows, gathered_ids, gathered_scores = (
        lax.all_gather(tokens, "group", axis=0, tiled=True),
        lax.all_gather(expert_ids, "group", axis=0, tiled=True),
        lax.all_gather(route_scores, "group", axis=0, tiled=True),
    )
    route_share = route_weights(gathered_scores)
    arrived_count = gathered_rows.shape[0]
    local_ids = gathered_ids - lax.axis_index("group") * EXP_GROUP
    matches = local_ids[:, :, None] == jnp.arange(EXP_GROUP, dtype=jnp.int32)[None, None, :]
    routed = jnp.any(matches, axis=1)
    shares = jnp.sum(jnp.where(matches, route_share[:, :, None], 0.0), axis=1)
    row = jnp.arange(arrived_count, dtype=jnp.int32)
    earlier = (row[None, :] <= row[:, None])[:, :, None] & routed[None, :, :]
    ranking = jnp.sum(earlier.astype(jnp.int32), axis=1) - 1
    placing = routed[:, :, None] & (
        ranking[:, :, None] == jnp.arange(slot_count, dtype=jnp.int32)[None, None, :]
    )
    selector = placing.reshape(arrived_count, EXP_GROUP * slot_count).astype(jnp.bfloat16)
    per_expert = jnp.einsum(
        "rs,rd->sd", selector, gathered_rows, preferred_element_type=jnp.float32
    ).astype(jnp.bfloat16)
    shard_count = lax.axis_size("node") // EXP_GROUP
    outgoing = jnp.broadcast_to(
        per_expert.reshape(EXP_GROUP, 1, slot_count, width),
        (EXP_GROUP, shard_count, slot_count, width),
    ).reshape(EXP_GROUP * shard_count, slot_count, width)
    arrived = lax.all_to_all(outgoing, "node", split_axis=0, concat_axis=0, tiled=True)
    flat_rows = arrived.reshape(-1, width)
    produced = expert_dense(flat_rows, gate_weight, up_weight, down_weight)
    returned = lax.all_to_all(
        produced.reshape(arrived.shape), "node", split_axis=0, concat_axis=0, tiled=True
    )
    blocks = returned.reshape(EXP_GROUP, shard_count, slot_count, width)
    merged = jnp.zeros((EXP_GROUP, slot_count, width), jnp.float32)
    for shard_index in range(shard_count):
        merged = merged + blocks[:, shard_index].astype(jnp.float32)
    slot_index = jnp.clip(ranking, 0, slot_count - 1)
    group_rows = jnp.zeros((arrived_count, width), jnp.float32)
    for expert_local in range(EXP_GROUP):
        looked = merged[expert_local][slot_index[:, expert_local]]
        group_rows = group_rows + shares[:, expert_local][:, None] * looked
    summed = lax.psum_scatter(group_rows, "group", scatter_dimension=0, tiled=True)
    return summed.astype(jnp.bfloat16)


LANES = 128
CORES = 2
SIDE = 2
GROUPS_PER_TOKEN = 4
MESH = pl.DeviceIdType.MESH
ACROSS = (
    (0, 1, 1), (0, 1, 0), (0, 0, 1), (0, 0, 0), (1, 1, 1), (1, 1, 0), (1, 0, 1), (1, 0, 0),
)
BESIDE = ((2, 1, 1), (2, 1, 0), (2, 0, 1), (2, 0, 0), (3, 1, 1), (3, 1, 0), (3, 0, 1))
BESIDE_FIRST = 4


def dense_kernel(
    groups, nodes,
    tokens_hbm, ids_hbm, scores_hbm, gate_hbm, up_hbm, down_hbm, out_ref,
    tokens_ref, ids_ref, scores_ref, gate_vmem, up_vmem, down_vmem,
    arrived, outgoing, mate, summed, returned, planes, rows_ref, shares_ref,
    weight_sems, small_sems, token_send, token_recv, own_recv, share_recv,
    swap_sems, part_send, part_recv, own_part_recv,
):
    devices = groups * nodes
    places = nodes // CORES
    chips = groups * places
    half = chips // 2
    width = tokens_hbm.shape[1]
    lines = width // LANES
    group, node = lax.axis_index("group"), lax.axis_index("node")
    place, core = node // CORES, lax.rem(node, CORES)
    row, column = place // SIDE, lax.rem(place, SIDE)
    chip = group * places + place
    me = group * nodes + node
    sibling = (group, node + 1 - 2 * core)
    low = (groups - 1 - group) // 2
    levels = (3 * low, 1 + low, low * (1 - group) + (1 - low) * (5 - group), group)
    hub_start = (core * low + (1 - core) * (1 - low)) * chips
    other_start = (core * (1 - low) + (1 - core) * low) * chips

    def locate(code):
        rank, turn_row, turn_column = code
        other_row = row + turn_row - 2 * row * turn_row
        other_column = column + turn_column - 2 * column * turn_column
        return levels[rank], other_row * SIDE + other_column

    across = [locate(code) for code in ACROSS]
    beside = [locate(code) for code in BESIDE]

    def device(spot, other_core):
        return (spot[0], spot[1] * CORES + other_core)

    def seat(spot):
        return lax.rem(spot[0] * places + spot[1], half)

    def by_core(second, first):
        pl.when(core == 1)(second)
        pl.when(core == 0)(first)

    weight_copies = (
        pltpu.make_async_copy(gate_hbm.at[0], gate_vmem, weight_sems.at[0]),
        pltpu.make_async_copy(up_hbm.at[0], up_vmem, weight_sems.at[1]),
        pltpu.make_async_copy(down_hbm.at[0], down_vmem, weight_sems.at[2]),
    )

    barrier = pltpu.get_barrier_semaphore()

    def greet(targets):
        for target in targets:
            pl.semaphore_signal(barrier, inc=1, device_id=target, device_id_type=MESH)

    greet([device(spot, 1) for spot in across])
    by_core(
        lambda: greet([device(spot, 0) for spot in across]),
        lambda: greet([device(spot, 1) for spot in beside]))
    greet([device(spot, 0) for spot in beside] + [sibling])
    greeted = 2 * (chips - 1 - half) + half + 1 + core

    small_copies = (
        pltpu.make_async_copy(tokens_hbm, tokens_ref, small_sems.at[0]),
        pltpu.make_async_copy(ids_hbm, ids_ref, small_sems.at[1]),
        pltpu.make_async_copy(scores_hbm, scores_ref, small_sems.at[2]),
    )
    for copy in small_copies:
        copy.start()
    weight_copies[0].start(priority=1)
    weight_copies[1].start(priority=1)
    for copy in small_copies:
        copy.wait()

    own = tokens_ref[...].astype(jnp.float32)
    for line in range(lines):
        planes[line:line + 1, :] = own[:, line * LANES:(line + 1) * LANES]
    arrived[me] = planes[0:lines, :].astype(jnp.bfloat16)

    sigmoids = 1.0 / (1.0 + jnp.exp(-scores_ref[...].astype(jnp.float32)))
    weights = ROUTE_SCALE * sigmoids / jnp.sum(sigmoids, axis=1, keepdims=True)
    top = ids_ref.shape[1]
    chip_expert = lax.broadcasted_iota(jnp.int32, (chips, top), 0) // (nodes // EXP_GROUP // CORES)
    named = jnp.broadcast_to(ids_ref[...], (chips, top)) == chip_expert
    shares = jnp.sum(
        jnp.where(named, jnp.broadcast_to(weights, (chips, top)), 0.0), axis=1, keepdims=True)
    shares_ref[...] = jnp.broadcast_to(shares, (chips, LANES))

    pl.semaphore_wait(barrier, greeted)

    def send_tokens(ref, receive, target):
        pltpu.make_async_remote_copy(
            src_ref=ref, dst_ref=ref, send_sem=token_send, recv_sem=receive,
            device_id=target, device_id_type=MESH).start()

    for spot in across:
        send_tokens(arrived.at[me], token_recv.at[lax.rem(chip, half)], device(spot, 1))
    for spot in beside:
        send_tokens(arrived.at[me], token_recv.at[lax.rem(chip, half)], device(spot, 0))
    send_tokens(arrived.at[me], own_recv, sibling)
    weight_copies[2].start(priority=1)

    def pass_on(spots):
        for spot in reversed(spots):
            pair = arrived.at[pl.ds((spot[0] * places + spot[1]) * CORES, CORES)]
            pltpu.make_async_copy(pair, pair, token_recv.at[seat(spot)]).wait()
            send_tokens(pair, share_recv, sibling)

    by_core(lambda: pass_on(across), lambda: pass_on(beside))

    def wait_for(ref, semaphore):
        pltpu.make_async_copy(ref, ref, semaphore).wait()

    def lay_out(first, start):
        planes[first * lines:(first + chips) * lines, :] = arrived[
            pl.ds(start, chips)].astype(jnp.float32).reshape(chips * lines, LANES)
        for line in range(lines):
            rows_ref[first:first + chips, line * LANES:(line + 1) * LANES] = planes[
                pl.ds(first * lines + line, chips, stride=lines), :].astype(jnp.bfloat16)

    def product(left, right):
        return jnp.dot(left, right, preferred_element_type=jnp.float32)

    def front(first):
        rows = rows_ref[first:first + chips, :]
        gate_pre, up_proj = product(rows, gate_vmem[...]), product(rows, up_vmem[...])
        return (gate_pre / (1.0 + jnp.exp(-gate_pre)) * up_proj).astype(jnp.bfloat16)

    def back(first, hidden):
        produced = product(hidden, down_vmem[...])
        for line in range(lines):
            planes[pl.ds(first * lines + line, chips, stride=lines), :] = produced[:, line * LANES:(line + 1) * LANES]

    wait_for(arrived.at[0], own_recv)
    lay_out(0, hub_start)
    weight_copies[0].wait()
    weight_copies[1].wait()
    hub_hidden = front(0)
    by_core(
        lambda: wait_for(arrived.at[pl.ds(0, chips - CORES)], share_recv),
        lambda: wait_for(arrived.at[pl.ds(0, chips)], share_recv))
    lay_out(chips, other_start)
    other_hidden = front(chips)
    weight_copies[2].wait()
    back(chips, other_hidden)
    outgoing[...] = planes[chips * lines:2 * chips * lines, :].astype(jnp.bfloat16).reshape(chips, lines, LANES)
    def swap_part(index, start):
        piece = pl.ds(start, half)
        return pltpu.make_async_remote_copy(
            src_ref=outgoing.at[piece], dst_ref=mate.at[piece],
            send_sem=swap_sems.at[0, index], recv_sem=swap_sems.at[1, index],
            device_id=sibling, device_id_type=MESH)

    first_piece = (1 - core) * lax.rem(levels[0], 2) * half + core * lax.rem(levels[2], 2) * half
    got_first = core * lax.rem(levels[0], 2) * half + (1 - core) * lax.rem(levels[2], 2) * half
    swaps = (swap_part(0, first_piece), swap_part(1, half - first_piece))
    arrivals = (swap_part(0, got_first), swap_part(1, half - got_first))
    swaps[0].start()
    swaps[1].start()
    back(0, hub_hidden)
    arrivals[0].wait_recv()

    def add_up(base, count):
        begin = pl.multiple_of(base * lines, lines)
        return (
            planes[pl.ds(begin, count * lines), :].reshape(count, lines, LANES)
            + mate[pl.ds(base, count)].astype(jnp.float32)).astype(jnp.bfloat16)

    def send_part(index, receive, target):
        pltpu.make_async_remote_copy(
            src_ref=summed.at[index], dst_ref=returned.at[chip],
            send_sem=part_send, recv_sem=receive,
            device_id=target, device_id_type=MESH).start()

    def give_back(spots, more):
        for index, spot in enumerate(spots):
            if index == more:
                arrivals[1].wait_recv()
            base = seat(spot) * CORES
            summed[pl.ds(base, CORES)] = add_up(base, CORES)
            for other_core in range(CORES):
                send_part(base + other_core, part_recv, device(spot, other_core))

    def give_back_beside():
        give_back(beside, BESIDE_FIRST)
        base = lax.rem(chip, half) * CORES
        summed[pl.ds(base, CORES)] = add_up(base, CORES)
        send_part(base + 1, own_part_recv, sibling)
        returned[chip] = summed[base]

    by_core(lambda: give_back(across, places), give_back_beside)
    wait_for(returned.at[pl.ds(0, chips - 1)], part_recv)
    pl.when(core == 1)(lambda: wait_for(returned.at[0], own_part_recv))
    total = jnp.zeros((lines, LANES), jnp.float32)
    for source in range(chips):
        total += shares_ref[source:source + 1, :] * returned[source].astype(jnp.float32)
    out_ref[...] = total.astype(jnp.bfloat16)
    swaps[0].wait_send()
    swaps[1].wait_send()

    def drain(tokens_sent, parts_sent):
        wait_for(arrived.at[pl.ds(0, tokens_sent)], token_send)
        wait_for(returned.at[pl.ds(0, parts_sent)], part_send)

    by_core(lambda: drain(devices, chips), lambda: drain(devices - CORES, chips - 1))


def per_device_dense(groups, nodes, tokens, expert_ids, route_scores, gate_weight, up_weight, down_weight):
    devices = groups * nodes
    chips = devices // CORES
    width = tokens.shape[1]
    hidden_size = gate_weight.shape[2]
    lines = width // LANES
    parts = pltpu.VMEM((chips, lines, LANES), jnp.bfloat16)
    in_hbm = pl.BlockSpec(memory_space=pltpu.HBM)
    dma = pltpu.SemaphoreType.DMA
    out = pl.pallas_call(
        functools.partial(dense_kernel, groups, nodes),
        out_shape=jax.ShapeDtypeStruct((lines, LANES), jnp.bfloat16),
        in_specs=[in_hbm] * 6,
        out_specs=pl.BlockSpec(memory_space=pltpu.VMEM),
        scratch_shapes=[
            pltpu.VMEM(tokens.shape, tokens.dtype),
            pltpu.VMEM(expert_ids.shape, expert_ids.dtype),
            pltpu.VMEM(route_scores.shape, route_scores.dtype),
            pltpu.VMEM((width, hidden_size), jnp.bfloat16),
            pltpu.VMEM((width, hidden_size), jnp.bfloat16),
            pltpu.VMEM((hidden_size, width), jnp.bfloat16),
            pltpu.VMEM((devices, lines, LANES), jnp.bfloat16),
            parts, parts, parts, parts,
            pltpu.VMEM((devices * lines, LANES), jnp.float32),
            pltpu.VMEM((devices, width), jnp.bfloat16),
            pltpu.VMEM((chips, LANES), jnp.float32),
            dma((3,)), dma((3,)), dma, dma((chips // 2,)), dma, dma, dma((2, 2)), dma, dma, dma,
        ],
        compiler_params=pltpu.CompilerParams(
            collective_id=0, has_side_effects=True, vmem_limit_bytes=48 * 1024 * 1024),
    )(*(pltpu.with_memory_space_constraint(x, pltpu.HBM)
        for x in (tokens, expert_ids, route_scores, gate_weight, up_weight, down_weight)))
    return out.reshape(1, width)


def solution(mesh):
    groups, nodes = mesh.shape["group"], mesh.shape["node"]
    everyone = groups == GROUPS_PER_TOKEN and nodes == CORES * SIDE * SIDE
    body = functools.partial(per_device_dense, groups, nodes) if everyone else per_device
    return jax.shard_map(
        body,
        mesh=mesh,
        in_specs=(
            P(("group", "node"), None),
            P(("group", "node"), None),
            P(("group", "node"), None),
            P(("group", "node"), None, None),
            P(("group", "node"), None, None),
            P(("group", "node"), None, None),
        ),
        out_specs=P(("group", "node"), None),
        check_vma=False,
    )
```
